32 devices in a mesh: dp: 8 (over z, y), tensor: 4 (over x, core).
Axes of the slice: x: 2, y: 2, z: 4, core: 2. Of those that a mesh axis runs over, the one named last changes fastest.
Arguments:
- hidden_in: bfloat16 [24576, 768], P(('dp', 'tensor')), may hold values from -6 to 6
- cotangent: bfloat16 [24576, 768], P(('dp', 'tensor')), may hold values from -6 to 6
- lengths: int32 [8, 2, 3], P('dp'), may hold values from 1 to 1024, 1536 in all within a row
- deal: int32 [24576], P('dp'), may hold values from 0 to 24575, as said below
- inverse: int32 [24576], P('dp'), may hold values from 0 to 24575, as said below
- micro: int32 [8, 2], P('dp'), may hold values from 0 to 1, as said below
- qkv_weight: float32 [2, 768, 3, 768], P(None, 'dp', None, 'tensor'), may hold values from -0.21875 to 0.21875
- proj_weight: float32 [2, 768, 768], P(None, 'dp', 'tensor'), may hold values from -2.5 to 2.5
- gate_up_weight: float32 [2, 768, 2, 3072], P(None, 'dp', None, 'tensor'), may hold values from -0.21875 to 0.21875
- down_weight: float32 [2, 768, 3072], P(None, 'dp', 'tensor'), may hold values from -0.109375 to 0.109375
- norm_params: float32 [2, 4, 768], replicated, may hold values from -0.9 to 1.45, as said below
- qkv_momentum: float32 [2, 768, 3, 768], P(None, 'dp', None, 'tensor'), may hold values from -256 to 256
- proj_momentum: float32 [2, 768, 768], P(None, 'dp', 'tensor'), may hold values from -256 to 256
- gate_up_momentum: float32 [2, 768, 2, 3072], P(None, 'dp', None, 'tensor'), may hold values from -256 to 256
- down_momentum: float32 [2, 768, 3072], P(None, 'dp', 'tensor'), may hold values from -256 to 256
- norm_momentum: float32 [2, 4, 768], replicated, may hold values from -896 to 896
- qkv_average: float32 [2, 768, 3, 768], P(None, 'dp', None, 'tensor'), may hold values from -0.21875 to 0.21875
- proj_average: float32 [2, 768, 768], P(None, 'dp', 'tensor'), may hold values from -2.5 to 2.5
- gate_up_average: float32 [2, 768, 2, 3072], P(None, 'dp', None, 'tensor'), may hold values from -0.21875 to 0.21875
- down_average: float32 [2, 768, 3072], P(None, 'dp', 'tensor'), may hold values from -0.109375 to 0.109375
- norm_average: float32 [2, 4, 768], replicated, may hold values from 0.5 to 1.5
Outputs:
- block_out: float32 [24576, 768], P(('dp', 'tensor'))
- input_grad: float32 [24576, 768], P(('dp', 'tensor'))
- qkv_grad: float32 [2, 768, 3, 768], P(None, 'dp', None, 'tensor')
- qkv_new: float32 [2, 768, 3, 768], P(None, 'dp', None, 'tensor')
- qkv_momentum_new: float32 [2, 768, 3, 768], P(None, 'dp', None, 'tensor')
- qkv_average_new: float32 [2, 768, 3, 768], P(None, 'dp', None, 'tensor')
- proj_grad: float32 [2, 768, 768], P(None, 'dp', 'tensor')
- proj_new: float32 [2, 768, 768], P(None, 'dp', 'tensor')
- proj_momentum_new: float32 [2, 768, 768], P(None, 'dp', 'tensor')
- proj_average_new: float32 [2, 768, 768], P(None, 'dp', 'tensor')
- gate_up_grad: float32 [2, 768, 2, 3072], P(None, 'dp', None, 'tensor')
- gate_up_new: float32 [2, 768, 2, 3072], P(None, 'dp', None, 'tensor')
- gate_up_momentum_new: float32 [2, 768, 2, 3072], P(None, 'dp', None, 'tensor')
- gate_up_average_new: float32 [2, 768, 2, 3072], P(None, 'dp', None, 'tensor')
- down_grad: float32 [2, 768, 3072], P(None, 'dp', 'tensor')
- down_new: float32 [2, 768, 3072], P(None, 'dp', 'tensor')
- down_momentum_new: float32 [2, 768, 3072], P(None, 'dp', 'tensor')
- down_average_new: float32 [2, 768, 3072], P(None, 'dp', 'tensor')
- norm_grad: float32 [2, 4, 768], replicated
- norm_new: float32 [2, 4, 768], replicated
- norm_momentum_new: float32 [2, 4, 768], replicated
- norm_average_new: float32 [2, 4, 768], replicated
The draws below stay inside these ranges and needn't reach their ends.
Inputs may be any that keep to these rules, and one draw needn't show every extreme that they name: deal is a permutation; slots of group g (rows g * 3072 to (g + 1) * 3072 - 1) take arrival rows of the same group. inverse[deal[s]] = s for every slot s. `micro`: each row is a permutation of the packs 0 to 1. `norm_params`: entries 0 and 2 of the second dimension are gains near 1, entries 1 and 3 biases near 0.
All inputs are finite; a program needn't handle non-finite values.
Results may differ from the reference program's by a relative error of at most 0.03.
The reference program's roundings to bfloat16 on the way count: a program that leaves them out, or rounds other values in their place, can miss the bound.
Values may be sent and summed in bfloat16 or wider, within the bound.
No kernel may reach another device: no remote copies, remote signals or barrier semaphores. Data moves between devices by JAX's collectives and lax.ppermute only.
A program may use at most 448 MiB of HBM per device.

```python
import math
import jax
import jax.numpy as jnp
import numpy as np
from jax import lax

D = 768
HEADS = 12
HEAD_DIM = 64
FF = 3072
L = 2
MB = 2
PACK = 1536
DOCS = 3
SEQ_MOST = 1024
GROUPS = 8
TOKENS = 24576


def dealing_pair(key):
    subkeys = jax.random.split(jax.random.fold_in(key, 11), GROUPS)
    group_rows = MB * PACK

    def permute_group(subkey):
        return jax.random.permutation(subkey, group_rows).astype(jnp.int32)
    perms = jax.vmap(permute_group)(subkeys)
    offsets = (jnp.arange(GROUPS, dtype=jnp.int32) * group_rows)[:, None]
    dealt = (perms + offsets).reshape(-1).astype(jnp.int32)
    reverted = jnp.zeros_like(dealt).at[dealt].set(jnp.arange(dealt.shape[0], dtype=jnp.int32))
    return (dealt, reverted)


def draw_deal(key, part):
    return dealing_pair(key)[0]


def draw_inverse(key, part):
    return dealing_pair(key)[1]


def draw_micro(key, part):
    subkeys = jax.random.split(jax.random.fold_in(key, 23), GROUPS)

    def permute_slots(subkey):
        return jax.random.permutation(subkey, MB).astype(jnp.int32)
    return jax.vmap(permute_slots)(subkeys).astype(jnp.int32)


def draw_norm_params(key, part):
    subkey = jax.random.fold_in(key, 31)
    spread = jnp.clip(jax.random.normal(subkey, (L, 4, D), jnp.float32), -3.0, 3.0)
    kinds = jnp.arange(4, dtype=jnp.int32)[None, :, None] % 2
    return jnp.where(kinds == 0, 1.0 + 0.15 * spread, 0.3 * spread).astype(jnp.float32)


def spiked(values, key, source, target, blocks, factor):
    owner, partner = [(jnp.arange(values.shape[dim]) // (values.shape[dim] // blocks)).reshape([-1 if axis == dim else 1 for axis in range(values.ndim)]) for dim in (source, target)]
    chosen = jax.random.permutation(key, blocks)[partner]
    strong = (owner == chosen) | (owner == (partner + blocks // 2) % blocks)
    return jnp.where(strong, factor * values, values)


def levels(stream_key, dims, shards, low, largest):
    def one(axis_at, parts):
        steps = jax.random.uniform(jax.random.fold_in(jax.random.fold_in(stream_key, 6), axis_at), (parts,), jnp.float32, low / len(shards), largest / len(shards))
        return jnp.repeat(jnp.exp(steps), dims[axis_at] // parts).reshape((-1,) + (1,) * (len(dims) - axis_at - 1))

    gain = one(*shards[0])
    for cut in shards[1:]:
        gain = gain * one(*cut)
    return gain


def length_profile(amount, total, most, slope):
    weights = [(1 << 20) // math.isqrt(standing ** slope) + 1 for standing in range(2, amount + 1)]
    spare, given = total - most - (amount - 1), [1] * (amount - 1)
    while spare > 0:
        free = [i for i in range(amount - 1) if given[i] < most]
        whole, budget = sum([weights[i] for i in free]), spare
        for i in free:
            extra = min(most - given[i], max(1, budget * weights[i] // whole), spare)
            given[i] = given[i] + extra
            spare = spare - extra
    return np.array([most] + given)


def ragged_sizes(rng, number_of, total, most, skew):
    if number_of == 2:
        one = jax.random.randint(rng, (), max(1, total - most), min(most, total - 1) + 1)
        return jnp.stack([one, total - one])
    sizes = jnp.asarray(length_profile(number_of, total, most, skew), jnp.int32)
    couples = (number_of - 1) // 2
    giver, taker = sizes[1:1 + 2 * couples:2], sizes[2:2 + 2 * couples:2]
    margin = jnp.minimum(giver - 1, most - taker)
    moved = jax.random.randint(jax.random.fold_in(rng, 1), (couples,), 0, 1 << 20) % (margin + 1)
    sizes = sizes.at[1:1 + 2 * couples:2].set(giver - moved).at[2:2 + 2 * couples:2].set(taker + moved)
    return sizes[jax.random.permutation(jax.random.fold_in(rng, 2), number_of)]


def noise(own_key, shape, scale, bound, cuts=(), held_as=jnp.bfloat16):
    gain = levels(own_key, shape, cuts, -0.22, 0.18) if cuts else 1.0
    drawn = jax.random.normal(own_key, shape, jnp.float32) * scale * gain
    return jnp.minimum(jnp.maximum(drawn, -bound), bound).astype(held_as)


def bell_draw_with(stream_key, extent, deviation, reach, shards, heavy, kind=jnp.bfloat16):
    values = deviation * jax.random.normal(stream_key, extent, jnp.float32)
    if shards:
        values = values * levels(stream_key, extent, shards, -0.22, 0.18)
    return jnp.clip(spiked(values, jax.random.fold_in(stream_key, 3), *heavy), -reach, reach).astype(kind)


def setup_inputs(seed: int = 0) -> dict:
    key_list = jax.random.split(jax.random.key(seed), 22)
    hidden_in = bell_draw_with(key_list[0], (TOKENS, D), 1.0, 6.0, ((0, 32),), (0, 1, 32, 2.75))
    cotangent = bell_draw_with(key_list[1], (TOKENS, D), 1.0, 6.0, ((0, 32),), (0, 1, 32, 2.75))
    lengths = jax.vmap(lambda own: ragged_sizes(own, DOCS, PACK, SEQ_MOST, 2))(jax.random.split(key_list[2], GROUPS * MB)).reshape((GROUPS, MB, DOCS)).astype(jnp.int32)
    deal = draw_deal(jax.random.fold_in(key_list[21], 71), 0)
    inverse = draw_inverse(jax.random.fold_in(key_list[21], 71), 0)
    micro = draw_micro(jax.random.fold_in(key_list[21], 71), 0)
    qkv_weight = noise(key_list[6], (L, D, 3, D), D ** -0.5, 0.21875, ((1, 8), (3, 4)), jnp.float32)
    proj_weight = noise(key_list[7], (L, D, D), (max(1, D * 8 // SEQ_MOST)) ** -0.5, 2.5, ((1, 8), (2, 4)), jnp.float32)
    gate_up_weight = noise(key_list[8], (L, D, 2, FF), D ** -0.5, 0.21875, ((1, 8), (3, 4)), jnp.float32)
    down_weight = noise(key_list[9], (L, D, FF), FF ** -0.5, 0.109375, ((1, 8), (2, 4)), jnp.float32)
    norm_params = draw_norm_params(jax.random.fold_in(key_list[21], 71), 0)
    qkv_momentum = noise(key_list[11], (L, D, 3, D), (0.3 * TOKENS ** 0.5), 256.0, ((1, 8), (3, 4)), jnp.float32)
    proj_momentum = noise(key_list[12], (L, D, D), (0.3 * TOKENS ** 0.5), 256.0, ((1, 8), (2, 4)), jnp.float32)
    gate_up_momentum = noise(key_list[13], (L, D, 2, FF), (0.3 * TOKENS ** 0.5), 256.0, ((1, 8), (3, 4)), jnp.float32)
    down_momentum = noise(key_list[14], (L, D, FF), (0.3 * TOKENS ** 0.5), 256.0, ((1, 8), (2, 4)), jnp.float32)
    norm_momentum = noise(key_list[15], (L, 4, D), (TOKENS ** 0.5), 896.0, (), jnp.float32)
    qkv_average = noise(key_list[16], (L, D, 3, D), D ** -0.5, 0.21875, ((1, 8), (3, 4)), jnp.float32)
    proj_average = noise(key_list[17], (L, D, D), (max(1, D * 8 // SEQ_MOST)) ** -0.5, 2.5, ((1, 8), (2, 4)), jnp.float32)
    gate_up_average = noise(key_list[18], (L, D, 2, FF), D ** -0.5, 0.21875, ((1, 8), (3, 4)), jnp.float32)
    down_average = noise(key_list[19], (L, D, FF), FF ** -0.5, 0.109375, ((1, 8), (2, 4)), jnp.float32)
    norm_average = jnp.clip(1.0 + 0.1 * jax.random.normal(key_list[20], (L, 4, D), jnp.float32), 0.5, 1.5)
    return dict(hidden_in=hidden_in, cotangent=cotangent, lengths=lengths, deal=deal, inverse=inverse, micro=micro, qkv_weight=qkv_weight, proj_weight=proj_weight, gate_up_weight=gate_up_weight, down_weight=down_weight, norm_params=norm_params, qkv_momentum=qkv_momentum, proj_momentum=proj_momentum, gate_up_momentum=gate_up_momentum, down_momentum=down_momentum, norm_momentum=norm_momentum, qkv_average=qkv_average, proj_average=proj_average, gate_up_average=gate_up_average, down_average=down_average, norm_average=norm_average)


norm_eps = 1e-05
rope_base = 1000.0
step_size = 2.0
norm_step = 0.1
keep_rate = 0.5
masked_value = -1e+30
highest = lax.Precision.HIGHEST

@jax.custom_vjp
def low(v):
    return lax.optimization_barrier(v.astype(jnp.bfloat16)).astype(jnp.float32)

@jax.custom_vjp
def low_back(v):
    return v

def low_keep(v):
    return (low(v), None)

def low_pass(kept, grad):
    return (grad,)

def back_keep(v):
    return (v, None)

def back_low(kept, grad):
    return (low(grad),)
low.defvjp(low_keep, low_pass)
low_back.defvjp(back_keep, back_low)

def documents(doc_lengths, pack_rows):
    doc_ends = jnp.cumsum(doc_lengths).astype(jnp.int32)
    row_ids = jnp.arange(pack_rows, dtype=jnp.int32)
    passed = (row_ids[:, None] >= doc_ends[None, :]).astype(jnp.int32)
    doc_ids = lax.optimization_barrier(jnp.sum(passed, axis=1))
    doc_starts = lax.optimization_barrier(jnp.sum(passed * doc_lengths[None, :].astype(jnp.int32), axis=1))
    return (doc_ids, (row_ids - doc_starts).astype(jnp.float32))

def rotary(positions, head_width):
    half_width = head_width // 2
    frequency = jnp.exp(jnp.arange(half_width, dtype=jnp.float32) * (-2.0 * math.log(rope_base) / head_width))
    angles = positions[:, None] * frequency[None, :]
    cosine = jnp.concatenate([jnp.cos(angles), jnp.cos(angles)], axis=1)[:, None, :]
    sine_table = jnp.concatenate([jnp.sin(angles), jnp.sin(angles)], axis=1)[:, None, :]
    return (cosine, sine_table)

def rotate(values, cosine, sine_table):
    half_width = values.shape[-1] // 2
    turned = jnp.concatenate([-values[..., half_width:], values[..., :half_width]], axis=-1)
    return values * cosine + turned * sine_table

def layer_norm(summed, gain_row, bias_row):
    row_mean = lax.optimization_barrier(jnp.mean(summed, axis=-1, keepdims=True))
    centred = summed - row_mean
    variance = lax.optimization_barrier(jnp.mean(centred * centred, axis=-1, keepdims=True))
    return centred * lax.rsqrt(variance + norm_eps) * gain_row + bias_row

def encoder_layer(inputs, qkv_mat, proj_mat, gate_mat, down_mat, norm_rows, cosine, sine_table, same_doc):
    row_count = inputs.shape[0]
    projected = low_back(jnp.einsum('rd,djc->rjc', low(inputs), low(qkv_mat), precision=highest))
    split_shape = (row_count, HEADS, HEAD_DIM)
    queries = low(rotate(projected[:, 0].reshape(split_shape), cosine, sine_table))
    key_rows = low(rotate(projected[:, 1].reshape(split_shape), cosine, sine_table))
    value_rows = low(projected[:, 2].reshape(split_shape))
    block_rows = min(512, row_count)
    scale = HEAD_DIM ** (-0.5)

    def attend(blocks):
        query_block, mask_block = blocks
        scores = low_back(jnp.einsum('qhd,khd->hqk', query_block, key_rows, precision=highest) * scale)
        scores = jnp.where(mask_block[None], scores, masked_value)
        probs_soft = jax.nn.softmax(scores, axis=-1)
        return jnp.einsum('hqk,khd->qhd', low(probs_soft), value_rows, precision=highest)
    block_count = row_count // block_rows
    attended = lax.map(jax.checkpoint(attend), (queries.reshape(block_count, block_rows, HEADS, HEAD_DIM), same_doc.reshape(block_count, block_rows, row_count)))
    attended = low(low_back(attended.reshape(row_count, D)))
    attn_out = low_back(jnp.einsum('rc,dc->rd', attended, low(proj_mat), precision=highest))
    middle = layer_norm(inputs + attn_out, norm_rows[0], norm_rows[1])
    gate_up = low_back(jnp.einsum('rd,djc->rjc', low(middle), low(gate_mat), precision=highest))
    hidden = low(low_back(jax.nn.silu(gate_up[:, 0]) * gate_up[:, 1]))
    ffn_out = low_back(jnp.einsum('rc,dc->rd', hidden, low(down_mat), precision=highest))
    return layer_norm(middle + ffn_out, norm_rows[2], norm_rows[3])

def forward(inputs, params, doc_lengths):
    doc_ids, positions = documents(doc_lengths, PACK)
    same_doc = doc_ids[:, None] == doc_ids[None, :]
    cosine, sine_table = rotary(positions, HEAD_DIM)
    qkv_all, proj_all, gate_all, down_all, norm_all = params
    for layer_idx in range(L):
        inputs = encoder_layer(inputs, qkv_all[layer_idx], proj_all[layer_idx], gate_all[layer_idx], down_all[layer_idx], norm_all[layer_idx], cosine, sine_table, same_doc)
    return inputs

def update(weight, gradient, moment, average, rate):
    moment_new = keep_rate * moment + gradient
    weight_new = weight - rate * (gradient + keep_rate * moment_new)
    average_new = keep_rate * average + (1.0 - keep_rate) * weight_new
    return (gradient, weight_new, moment_new, average_new)

def reference(hidden_in, cotangent, lengths, deal, inverse, micro, qkv_weight, proj_weight, gate_up_weight, down_weight, norm_params, qkv_momentum, proj_momentum, gate_up_momentum, down_momentum, norm_momentum, qkv_average, proj_average, gate_up_average, down_average, norm_average):
    dealt_in = hidden_in.astype(jnp.float32)[deal].reshape(GROUPS, MB, PACK, D)
    dealt_grad = cotangent.astype(jnp.float32)[deal].reshape(GROUPS, MB, PACK, D)
    chosen = micro[:, :, None, None]
    pack_inputs = jnp.take_along_axis(dealt_in, chosen, axis=1).reshape(GROUPS * MB, PACK, D)
    pack_grads = jnp.take_along_axis(dealt_grad, chosen, axis=1).reshape(GROUPS * MB, PACK, D)
    params = (qkv_weight, proj_weight, gate_up_weight, down_weight, norm_params)

    def one_pack(running, pack_item):
        inputs, pack_cot, doc_lengths = pack_item
        outputs, pullback = jax.vjp(lambda values, weights: forward(values, weights, doc_lengths), inputs, params)
        input_part, weight_parts = pullback(pack_cot)
        running = tuple((before + fresh for before, fresh in zip(running, weight_parts)))
        return (running, (outputs, input_part))
    starting = tuple((jnp.zeros_like(weight) for weight in params))
    sums, (pack_outs, pack_ins) = lax.scan(one_pack, starting, (pack_inputs, pack_grads, lengths.reshape(GROUPS * MB, DOCS)))
    matches = (micro[:, None, :] == jnp.arange(MB, dtype=jnp.int32)[None, :, None]).astype(jnp.int32)
    slot_of = lax.optimization_barrier(jnp.sum(matches * jnp.arange(MB, dtype=jnp.int32)[None, None, :], axis=2))
    ordered_out = jnp.take_along_axis(pack_outs.reshape(GROUPS, MB, PACK, D), slot_of[:, :, None, None], axis=1).reshape(TOKENS, D)
    ordered_in = jnp.take_along_axis(pack_ins.reshape(GROUPS, MB, PACK, D), slot_of[:, :, None, None], axis=1).reshape(TOKENS, D)
    block_out = ordered_out[inverse]
    input_grad = ordered_in[inverse]
    proj_fan = max(1, D * 8 // SEQ_MOST)
    qkv_state = update(qkv_weight, sums[0], qkv_momentum, qkv_average, step_size / math.sqrt(TOKENS * D))
    proj_state = update(proj_weight, sums[1], proj_momentum, proj_average, step_size / math.sqrt(TOKENS * proj_fan))
    gate_state = update(gate_up_weight, sums[2], gate_up_momentum, gate_up_average, step_size / math.sqrt(TOKENS * D))
    down_state = update(down_weight, sums[3], down_momentum, down_average, step_size / math.sqrt(TOKENS * FF))
    norm_state = update(norm_params, sums[4], norm_momentum, norm_average, norm_step / math.sqrt(TOKENS))
    return (block_out, input_grad, qkv_state[0], qkv_state[1], qkv_state[2], qkv_state[3], proj_state[0], proj_state[1], proj_state[2], proj_state[3], gate_state[0], gate_state[1], gate_state[2], gate_state[3], down_state[0], down_state[1], down_state[2], down_state[3], norm_state[0], norm_state[1], norm_state[2], norm_state[3])
```

```python
import functools
import math

import jax
import jax.numpy as jnp
from jax import lax
from jax.experimental import pallas as pl
from jax.experimental.pallas import tpu as pltpu
from jax.sharding import Mesh, PartitionSpec as P

D = 768
HEAD_DIM = 64
FF = 3072
SEQ_MOST = 1024

norm_eps = 1e-05
rope_base = 1000.0
step_size = 2.0
norm_step = 0.1
keep_rate = 0.5
SCALE2 = HEAD_DIM ** (-0.5) * math.log2(math.e)
NT = (((1,), (1,)), ((), ()))
NN = (((1,), (0,)), ((), ()))
TN = (((0,), (0,)), ((), ()))


def mm(a, b, dims):
    return lax.dot_general(a, b, dims, preferred_element_type=jnp.float32)


def attn_fwd_body(BQ, BK, lo_ref, hi_ref, q_ref, k_ref, v_ref, dq_ref, dk_ref, o_ref, lse_ref):
    R = q_ref.shape[0]
    lane = lax.broadcasted_iota(jnp.int32, (BQ, 128), 1)
    first = lane < HEAD_DIM
    zero = jnp.zeros((BQ, 128), jnp.bfloat16)

    def q_block(i, _):
        rows = pl.ds(pl.multiple_of(i * BQ, BQ), BQ)
        q = q_ref[rows, :]
        qs = (jnp.where(first, q, zero), jnp.where(first, zero, q))
        dq = dq_ref[rows, :]

        def kv_block(j, carry):
            cols = pl.ds(pl.multiple_of(j * BK, BK), BK)
            k = k_ref[cols, :]
            v = v_ref[cols, :]
            same = dq == dk_ref[:, cols]
            out = []
            for h in range(2):
                m, l, acc = carry[h]
                s = mm(qs[h], k, NT) * SCALE2
                s = jnp.where(same, s, -1e30)
                m_new = jnp.maximum(m, jnp.max(s, axis=1, keepdims=True))
                alpha = jnp.exp2(m - m_new)
                p = jnp.exp2(s - m_new)
                l = alpha * l + jnp.sum(p, axis=1, keepdims=True)
                acc = alpha * acc + mm(p.astype(jnp.bfloat16), v, NN)
                out.append((m_new, l, acc))
            return tuple(out)

        start = tuple(
            (jnp.full((BQ, 1), -2e30, jnp.float32), jnp.zeros((BQ, 1), jnp.float32), jnp.zeros((BQ, 128), jnp.float32))
            for h in range(2)
        )
        (m0, l0, a0), (m1, l1, a1) = lax.fori_loop(lo_ref[i], hi_ref[i], kv_block, start)
        o_ref[rows, :] = jnp.where(first, a0 / l0, a1 / l1).astype(jnp.bfloat16)
        lse_ref[rows, :] = jnp.where(first, m0 + jnp.log2(l0), m1 + jnp.log2(l1))
        return 0

    lax.fori_loop(0, R // BQ, q_block, 0)


def attn_fwd(lo, hi, q, k, v, dq, dk, BQ=256, BK=256):
    R, C = q.shape
    pairs = C // 128
    blk = pl.BlockSpec((R, 128), lambda p, *_: (0, p))
    return pl.pallas_call(
        functools.partial(attn_fwd_body, BQ, BK),
        out_shape=(jax.ShapeDtypeStruct((R, C), jnp.bfloat16), jax.ShapeDtypeStruct((R, C), jnp.float32)),
        grid_spec=pltpu.PrefetchScalarGridSpec(
            num_scalar_prefetch=2, grid=(pairs,),
            in_specs=[blk, blk, blk, pl.BlockSpec((R, 1), lambda p, *_: (0, 0)), pl.BlockSpec((1, R), lambda p, *_: (0, 0))],
            out_specs=[blk, blk]),
        cost_estimate=pl.CostEstimate(flops=pairs * 2 * R * R * 64 * 4, bytes_accessed=R * C * 12, transcendentals=pairs * 2 * R * R),
        name="attn_fwd",
    )(lo, hi, q, k, v, dq, dk)


def attn_bwd_body(BQ, BK, mode, lo_ref, hi_ref, q_ref, k_ref, v_ref, do_ref, o_ref, lse_ref, dq_ref, dk_ref,
                  gq_ref, gk_ref, gv_ref, gq_s, lse_s, delta_s):
    R = q_ref.shape[0]
    nq = R // BQ
    scale = HEAD_DIM ** (-0.5)
    gk_ref[...] = jnp.zeros((R, 128), jnp.float32)
    gv_ref[...] = jnp.zeros((R, 128), jnp.float32)
    fq = lax.broadcasted_iota(jnp.int32, (BQ, 128), 1) < HEAD_DIM
    fk = lax.broadcasted_iota(jnp.int32, (BK, 128), 1) < HEAD_DIM
    zq = jnp.zeros((BQ, 128), jnp.bfloat16)
    zk = jnp.zeros((BK, 128), jnp.bfloat16)

    def q_block(i, _):
        rows = pl.ds(pl.multiple_of(i * BQ, BQ), BQ)
        q = q_ref[rows, :]
        do = do_ref[rows, :]
        prod = do.astype(jnp.float32) * o_ref[rows, :].astype(jnp.float32)
        lse_t = lse_ref[rows, :].T
        prod_t = prod.T
        qs = (jnp.where(fq, q, zq), jnp.where(fq, zq, q))
        dos = (jnp.where(fq, do, zq), jnp.where(fq, zq, do))
        lses = (lse_t[0:1, :], lse_t[64:65, :])
        deltas = (jnp.sum(prod_t[:64, :], axis=0, keepdims=True), jnp.sum(prod_t[64:, :], axis=0, keepdims=True))
        dq = dq_ref[:, rows]

        def kv_block(j, acc):
            cols = pl.ds(pl.multiple_of(j * BK, BK), BK)
            k = k_ref[cols, :]
            v = v_ref[cols, :]
            same = dk_ref[cols, :] == dq
            gk = gk_ref[cols, :]
            gv = gv_ref[cols, :]
            ks = (jnp.where(fk, k, zk), jnp.where(fk, zk, k))
            for h in range(2):
                s = mm(k, qs[h], NT) * SCALE2
                p = jnp.exp2(jnp.where(same, s - lses[h], -1e30))
                dp = mm(v, dos[h], NT)
                ds = (p * (dp - deltas[h])).astype(jnp.bfloat16)
                gv = gv + mm(p.astype(jnp.bfloat16), dos[h], NN)
                gk = gk + mm(ds, qs[h], NN)
                acc = acc + mm(ds, ks[h], TN)
            gk_ref[cols, :] = gk
            gv_ref[cols, :] = gv
            return acc

        gq_ref[rows, :] = lax.fori_loop(lo_ref[i], hi_ref[i], kv_block, jnp.zeros((BQ, 128), jnp.float32)) * scale
        return 0

    lax.fori_loop(0, nq, q_block, 0)
    gk_ref[...] = gk_ref[...] * scale


def attn_bwd(lo, hi, q, k, v, do, o, lse, dqrow, dkcol, BQ=256, BK=256, mode=0):
    R, C = q.shape
    pairs = C // 128
    blk = pl.BlockSpec((R, 128), lambda p, *_: (0, p))
    f32 = jax.ShapeDtypeStruct((R, C), jnp.float32)
    return pl.pallas_call(
        functools.partial(attn_bwd_body, BQ, BK, mode),
        out_shape=(f32, f32, f32),
        grid_spec=pltpu.PrefetchScalarGridSpec(
            num_scalar_prefetch=2, grid=(pairs,),
            in_specs=[blk] * 6 + [pl.BlockSpec((1, R), lambda p, *_: (0, 0)), pl.BlockSpec((R, 1), lambda p, *_: (0, 0))],
            out_specs=[blk, blk, blk],
            scratch_shapes=[pltpu.VMEM((8, 128), jnp.float32)] * 3),
        cost_estimate=pl.CostEstimate(flops=pairs * 2 * R * R * 64 * 10, bytes_accessed=R * C * 24, transcendentals=pairs * 2 * R * R),
        name="attn_bwd",
    )(lo, hi, q, k, v, do, o, lse, dqrow, dkcol)


def ranges(lens, R, BQ, BK):
    ends = jnp.cumsum(lens)
    rid = jnp.arange(R)
    passed = (rid[:, None] >= ends[None, :]).astype(jnp.int32)
    doc = jnp.sum(passed, 1)
    st = jnp.sum(passed * lens[None, :], 1)
    en = jnp.sum(jnp.where(doc[:, None] == jnp.arange(lens.shape[0])[None, :], ends[None, :], 0), 1)
    lo = st[::BQ] // BK
    hi = (en[BQ - 1::BQ] + BK - 1) // BK
    return doc, (rid - st).astype(jnp.float32), lo.astype(jnp.int32), hi.astype(jnp.int32)


F32 = jnp.float32
BF16 = jnp.bfloat16
SWAP = [(0, 1), (1, 0)]


def swap(values, axis):
    return lax.ppermute(values, axis, SWAP)


def rope_tables(positions):
    lane = jnp.arange(128, dtype=jnp.int32)
    frequency = jnp.exp((lane % 32).astype(F32) * (-2.0 * math.log(rope_base) / HEAD_DIM))
    angles = positions[:, None] * frequency[None, :]
    sign = jnp.where(lane % 64 < 32, -1.0, 1.0).astype(F32)
    return jnp.cos(angles), jnp.sin(angles) * sign[None, :]


def rotate(values, cosine, sine):
    rows, width = values.shape
    parts = values.reshape(rows, width // 64, 2, 32)
    turned = jnp.stack([parts[:, :, 1], parts[:, :, 0]], axis=2).reshape(rows, width)
    tiles = width // 128
    return values * jnp.tile(cosine, (1, tiles)) + turned * jnp.tile(sine, (1, tiles))


def layer_norm(summed, gain_row, bias_row):
    centred = summed - jnp.mean(summed, axis=-1, keepdims=True)
    inv_std = lax.rsqrt(jnp.mean(centred * centred, axis=-1, keepdims=True) + norm_eps)
    normed = centred * inv_std
    return (normed * gain_row + bias_row, normed, inv_std)


def norm_back(grad_out, normed, inv_std, gain_row):
    e = grad_out * gain_row
    return inv_std * (
        e - jnp.mean(e, axis=-1, keepdims=True) - normed * jnp.mean(e * normed, axis=-1, keepdims=True)
    )


def dot(a, b, dims):
    return lax.dot_general(a, b, (dims, ((), ())), preferred_element_type=F32)


def both(partial):
    partial = partial.astype(BF16)
    other = swap(partial, "core")
    return partial.astype(F32) + other.astype(F32)


def forward_layer(x, xb, mats, norm_rows, tables, ids):
    wq, wo, wg, wd = mats
    lo, hi, col, row = ids
    width = wo.shape[1]
    projected = dot(xb, wq, ((1,), (0,)))
    q = rotate(projected[:, :width], *tables).astype(BF16)
    k = rotate(projected[:, width : 2 * width], *tables).astype(BF16)
    v = projected[:, 2 * width :].astype(BF16)
    o, lse = attn_fwd(lo, hi, q, k, v, col, row, 512, 512)
    a = both(dot(o, wo, ((1,), (1,))))
    h, n1, r1 = layer_norm(x + a, norm_rows[0], norm_rows[1])
    hb = h.astype(BF16)
    half = wd.shape[1]
    gate_up = dot(hb, wg, ((1,), (0,)))
    m = (jax.nn.silu(gate_up[:, :half]) * gate_up[:, half:]).astype(BF16)
    f = both(dot(m, wd, ((1,), (1,))))
    y, n2, r2 = layer_norm(h + f, norm_rows[2], norm_rows[3])
    return (xb, q, k, v, o, lse, n1, r1, hb, gate_up, m, n2, r2), y


def backward_layer(dy, mats, norm_rows, kept, tables, ids):
    xb, q, k, v, o, lse, n1, r1, hb, gate_up, m, n2, r2 = kept
    wq, wo, wg, wd = mats
    lo, hi, col, row = ids
    half = wd.shape[1]
    gain2 = jnp.sum(dy * n2, axis=0)
    bias2 = jnp.sum(dy, axis=0)
    dz2 = norm_back(dy, n2, r2, norm_rows[2])
    dzb2 = dz2.astype(BF16)
    g_down = dot(dzb2, m, ((0,), (0,)))
    dm = dot(dzb2, wd, ((1,), (0,)))
    gate, up = gate_up[:, :half], gate_up[:, half:]
    sig = jax.nn.sigmoid(gate)
    dub = jnp.concatenate(
        [dm * up * sig * (1.0 + gate * (1.0 - sig)), dm * gate * sig], axis=1
    ).astype(BF16)
    g_gate = dot(hb, dub, ((0,), (0,)))
    dh = both(dot(dub, wg, ((1,), (1,)))) + dz2
    gain1 = jnp.sum(dh * n1, axis=0)
    bias1 = jnp.sum(dh, axis=0)
    dz1 = norm_back(dh, n1, r1, norm_rows[0])
    dzb1 = dz1.astype(BF16)
    g_proj = dot(dzb1, o, ((0,), (0,)))
    do = dot(dzb1, wo, ((1,), (0,))).astype(BF16)
    gq, gk, gv = attn_bwd(lo, hi, q, k, v, do, o, lse, row, col, 512, 512)
    cosine, sine = tables
    dpb = jnp.concatenate([rotate(gq, cosine, -sine), rotate(gk, cosine, -sine), gv], axis=1).astype(BF16)
    g_qkv = dot(xb, dpb, ((0,), (0,)))
    dx = both(dot(dpb, wq, ((1,), (1,)))) + dz1
    return (g_qkv, g_proj, g_gate, g_down), jnp.stack([gain1, bias1, gain2, bias2]), dx


def update(weight, gradient, moment, average, rate):
    moment_new = keep_rate * moment + gradient
    weight_new = weight - rate * (gradient + keep_rate * moment_new)
    average_new = keep_rate * average + (1.0 - keep_rate) * weight_new
    return (gradient, weight_new, moment_new, average_new)


def gather(shard, splits):
    rows, cols = shard.shape
    whole = lax.all_gather(shard, ("dp", "tx"), axis=0, tiled=True)
    return whole.reshape(-1, splits, rows, cols).transpose(1, 0, 2, 3).reshape(splits, -1, cols)


def scatter(parts, rows):
    splits, _, cols = parts.shape
    laid = parts.astype(BF16).reshape(splits, -1, rows, cols).transpose(1, 0, 2, 3).reshape(-1, cols)
    return lax.psum_scatter(laid, ("dp", "tx"), scatter_dimension=0, tiled=True).astype(F32)


def per_device(
    hidden_in, cotangent, lengths, deal, inverse, micro,
    qkv_weight, proj_weight, gate_up_weight, down_weight, norm_params,
    qkv_momentum, proj_momentum, gate_up_momentum, down_momentum, norm_momentum,
    qkv_average, proj_average, gate_up_average, down_average, norm_average,
):
    layers, rows = qkv_weight.shape[:2]
    heads_w = proj_weight.shape[2]
    hid_w = down_weight.shape[2]
    batches = micro.shape[1]
    local_rows, width = hidden_in.shape
    group_rows = deal.shape[0]
    pack_rows = group_rows // batches
    tx = lax.axis_index("tx")
    core = lax.axis_index("core")
    group_base = lax.axis_index("dp") * group_rows

    def four(block):
        pair = jnp.concatenate([block, swap(block, "tx")], axis=0)
        return jnp.concatenate([pair, swap(pair, "core")], axis=0)

    pack = lax.dynamic_index_in_dim(micro[0], tx, 0, keepdims=False)
    wanted = lax.dynamic_slice_in_dim(deal, pack * pack_rows, pack_rows, 0) - group_base
    block = wanted // local_rows
    place = jnp.where(block % 2 != core, 2, 0) + jnp.where(block // 2 != tx, 1, 0)
    source = place * local_rows + wanted % local_rows
    xb = four(hidden_in)[source]

    lens = lax.dynamic_index_in_dim(lengths[0], tx, 0, keepdims=False)
    doc, positions, lo, hi = ranges(lens, pack_rows, 512, 512)
    ids = (lo, hi, doc[:, None], doc[None, :])
    tables = rope_tables(positions)

    mats = []
    for i in range(layers):
        shard_a = jnp.concatenate(
            [qkv_weight[i].reshape(rows, 3 * heads_w), proj_weight[i]], axis=1
        ).astype(BF16)
        shard_b = jnp.concatenate(
            [gate_up_weight[i].reshape(rows, 2 * hid_w), down_weight[i]], axis=1
        ).astype(BF16)
        wa = gather(shard_a, 2)
        wb = gather(shard_b, 2)

        def side(w, first, count, each):
            return jnp.concatenate(
                [w[t][:, (first + c) * each : (first + c + 1) * each] for c in range(count) for t in range(2)], axis=1
            )

        mats.append((
            side(wa, 0, 3, heads_w), side(wa, 3, 1, heads_w), side(wb, 0, 2, hid_w), side(wb, 2, 1, hid_w)
        ))

    x = xb.astype(F32)
    stash = []
    for i in range(layers):
        kept, x = forward_layer(x, xb, mats[i], norm_params[i], tables, ids)
        xb = x.astype(BF16)
        stash.append(kept)

    def arrivals(values):
        half = pack_rows // 2
        mine = lax.dynamic_slice_in_dim(values, core * half, half, 0)
        far = swap(mine, "tx")
        near = swap(far, "core")
        other = jnp.where(core == 0, jnp.concatenate([far, near]), jnp.concatenate([near, far]))
        slots = lax.dynamic_slice_in_dim(inverse, (tx * 2 + core) * local_rows, local_rows, 0) - group_base
        held = slots // pack_rows == pack
        at = jnp.where(held, 0, pack_rows) + slots % pack_rows
        return jnp.concatenate([values, other])[at].astype(F32)

    block_out = arrivals(xb)

    grad = four(cotangent)[source].astype(F32)
    shares = [None] * layers
    norm_sums = [None] * layers
    for i in range(layers - 1, -1, -1):
        (g_qkv, g_proj, g_gate, g_down), norm_sums[i], grad = backward_layer(
            grad, mats[i], norm_params[i], stash[i], tables, ids
        )

        def sides(g, count, each):
            return [
                jnp.concatenate([g[:, (2 * c + t) * each : (2 * c + t + 1) * each] for c in range(count)], axis=1)
                for t in range(2)
            ]

        gu, dn = sides(g_gate, 2, hid_w), sides(g_down, 1, hid_w)
        qk, pr = sides(g_qkv, 3, heads_w), sides(g_proj, 1, heads_w)
        share_b = scatter(jnp.stack([jnp.concatenate([gu[t], dn[t]], axis=1) for t in range(2)]), rows)
        share_a = scatter(jnp.stack([jnp.concatenate([qk[t], pr[t]], axis=1) for t in range(2)]), rows)
        shares[i] = (
            share_a[:, : 3 * heads_w].reshape(rows, 3, heads_w),
            share_a[:, 3 * heads_w :],
            share_b[:, : 2 * hid_w].reshape(rows, 2, hid_w),
            share_b[:, 2 * hid_w :],
        )
    input_grad = arrivals(grad.astype(BF16))
    norm_total = lax.psum(0.5 * jnp.stack(norm_sums), ("dp", "tx", "core"))

    total_tokens = local_rows * lax.axis_size("dp") * lax.axis_size("tx") * lax.axis_size("core")
    proj_fan = max(1, D * 8 // SEQ_MOST)
    grads = [jnp.stack([shares[i][w] for i in range(layers)]) for w in range(4)]
    states = (
        update(qkv_weight, grads[0], qkv_momentum, qkv_average, step_size / math.sqrt(total_tokens * D)),
        update(proj_weight, grads[1], proj_momentum, proj_average, step_size / math.sqrt(total_tokens * proj_fan)),
        update(gate_up_weight, grads[2], gate_up_momentum, gate_up_average, step_size / math.sqrt(total_tokens * D)),
        update(down_weight, grads[3], down_momentum, down_average, step_size / math.sqrt(total_tokens * FF)),
        update(norm_params, norm_total, norm_momentum, norm_average, norm_step / math.sqrt(total_tokens)),
    )
    return (block_out, input_grad) + tuple(v for s in states for v in s)


def solution(mesh):
    dp, tensor = mesh.devices.shape
    fine = Mesh(mesh.devices.reshape(dp, 2, tensor // 2), ("dp", "tx", "core"))
    T = ("tx", "core")
    row = P(("dp",) + T, None)
    w4 = P(None, "dp", None, T)
    w3 = P(None, "dp", T)
    state = (w4, w3, w4, w3, P())
    placed = (row, row, P("dp", None, None), P("dp"), P("dp"), P("dp", None)) + state * 3
    outs = (row, row) + (w4,) * 4 + (w3,) * 4 + (w4,) * 4 + (w3,) * 4 + (P(),) * 4
    return jax.shard_map(per_device, mesh=fine, in_specs=placed, out_specs=outs, check_vma=False)
```

```python
import functools
import math

import jax
import jax.numpy as jnp
from jax import lax
from jax.experimental import pallas as pl
from jax.experimental.pallas import tpu as pltpu
from jax.sharding import Mesh, PartitionSpec as P

D = 768
HEAD_DIM = 64
FF = 3072
SEQ_MOST = 1024

norm_eps = 1e-05
rope_base = 1000.0
step_size = 2.0
norm_step = 0.1
keep_rate = 0.5
SCALE2 = HEAD_DIM ** (-0.5) * math.log2(math.e)
NT = (((1,), (1,)), ((), ()))
NN = (((1,), (0,)), ((), ()))
TN = (((0,), (0,)), ((), ()))


def mm(a, b, dims):
    return lax.dot_general(a, b, dims, preferred_element_type=jnp.float32)


def attn_fwd_body(BQ, BK, lo_ref, hi_ref, q_ref, k_ref, v_ref, dq_ref, dk_ref, o_ref, lse_ref):
    R = q_ref.shape[0]
    lane = lax.broadcasted_iota(jnp.int32, (BQ, 128), 1)
    first = lane < HEAD_DIM
    zero = jnp.zeros((BQ, 128), jnp.bfloat16)

    def q_block(i, _):
        rows = pl.ds(pl.multiple_of(i * BQ, BQ), BQ)
        q = q_ref[rows, :]
        qs = (jnp.where(first, q, zero), jnp.where(first, zero, q))
        dq = dq_ref[rows, :]

        def kv_block(j, carry):
            cols = pl.ds(pl.multiple_of(j * BK, BK), BK)
            k = k_ref[cols, :]
            v = v_ref[cols, :]
            same = dq == dk_ref[:, cols]
            out = []
            for h in range(2):
                m, l, acc = carry[h]
                s = mm(qs[h], k, NT) * SCALE2
                s = jnp.where(same, s, -1e30)
                m_new = jnp.maximum(m, jnp.max(s, axis=1, keepdims=True))
                alpha = jnp.exp2(m - m_new)
                p = jnp.exp2(s - m_new)
                l = alpha * l + jnp.sum(p, axis=1, keepdims=True)
                acc = alpha * acc + mm(p.astype(jnp.bfloat16), v, NN)
                out.append((m_new, l, acc))
            return tuple(out)

        start = tuple(
            (jnp.full((BQ, 1), -2e30, jnp.float32), jnp.zeros((BQ, 1), jnp.float32), jnp.zeros((BQ, 128), jnp.float32))
            for h in range(2)
        )
        (m0, l0, a0), (m1, l1, a1) = lax.fori_loop(lo_ref[i], hi_ref[i], kv_block, start)
        o_ref[rows, :] = jnp.where(first, a0 / l0, a1 / l1).astype(jnp.bfloat16)
        lse_ref[rows, :] = jnp.where(first, m0 + jnp.log2(l0), m1 + jnp.log2(l1))
        return 0

    lax.fori_loop(0, R // BQ, q_block, 0)


def attn_fwd(lo, hi, q, k, v, dq, dk, BQ=256, BK=256):
    R, C = q.shape
    pairs = C // 128
    blk = pl.BlockSpec((R, 128), lambda p, *_: (0, p))
    return pl.pallas_call(
        functools.partial(attn_fwd_body, BQ, BK),
        out_shape=(jax.ShapeDtypeStruct((R, C), jnp.bfloat16), jax.ShapeDtypeStruct((R, C), jnp.float32)),
        grid_spec=pltpu.PrefetchScalarGridSpec(
            num_scalar_prefetch=2, grid=(pairs,),
            in_specs=[blk, blk, blk, pl.BlockSpec((R, 1), lambda p, *_: (0, 0)), pl.BlockSpec((1, R), lambda p, *_: (0, 0))],
            out_specs=[blk, blk]),
        cost_estimate=pl.CostEstimate(flops=pairs * 2 * R * R * 64 * 4, bytes_accessed=R * C * 12, transcendentals=pairs * 2 * R * R),
        name="attn_fwd",
    )(lo, hi, q, k, v, dq, dk)


def attn_bwd_body(BQ, BK, mode, lo_ref, hi_ref, q_ref, k_ref, v_ref, do_ref, o_ref, lse_ref, dq_ref, dk_ref,
                  gq_ref, gk_ref, gv_ref, gq_s, lse_s, delta_s):
    R = q_ref.shape[0]
    nq = R // BQ
    scale = HEAD_DIM ** (-0.5)
    gk_ref[...] = jnp.zeros((R, 128), jnp.float32)
    gv_ref[...] = jnp.zeros((R, 128), jnp.float32)
    fq = lax.broadcasted_iota(jnp.int32, (BQ, 128), 1) < HEAD_DIM
    fk = lax.broadcasted_iota(jnp.int32, (BK, 128), 1) < HEAD_DIM
    zq = jnp.zeros((BQ, 128), jnp.bfloat16)
    zk = jnp.zeros((BK, 128), jnp.bfloat16)

    def q_block(i, _):
        rows = pl.ds(pl.multiple_of(i * BQ, BQ), BQ)
        q = q_ref[rows, :]
        do = do_ref[rows, :]
        prod = do.astype(jnp.float32) * o_ref[rows, :].astype(jnp.float32)
        lse_t = lse_ref[rows, :].T
        prod_t = prod.T
        qs = (jnp.where(fq, q, zq), jnp.where(fq, zq, q))
        dos = (jnp.where(fq, do, zq), jnp.where(fq, zq, do))
        lses = (lse_t[0:1, :], lse_t[64:65, :])
        deltas = (jnp.sum(prod_t[:64, :], axis=0, keepdims=True), jnp.sum(prod_t[64:, :], axis=0, keepdims=True))
        dq = dq_ref[:, rows]

        def kv_block(j, acc):
            cols = pl.ds(pl.multiple_of(j * BK, BK), BK)
            k = k_ref[cols, :]
            v = v_ref[cols, :]
            same = dk_ref[cols, :] == dq
            gk = gk_ref[cols, :]
            gv = gv_ref[cols, :]
            ks = (jnp.where(fk, k, zk), jnp.where(fk, zk, k))
            for h in range(2):
                s = mm(k, qs[h], NT) * SCALE2
                p = jnp.exp2(jnp.where(same, s - lses[h], -1e30))
                dp = mm(v, dos[h], NT)
                ds = (p * (dp - deltas[h])).astype(jnp.bfloat16)
                gv = gv + mm(p.astype(jnp.bfloat16), dos[h], NN)
                gk = gk + mm(ds, qs[h], NN)
                acc = acc + mm(ds, ks[h], TN)
            gk_ref[cols, :] = gk
            gv_ref[cols, :] = gv
            return acc

        gq_ref[rows, :] = lax.fori_loop(lo_ref[i], hi_ref[i], kv_block, jnp.zeros((BQ, 128), jnp.float32)) * scale
        return 0

    lax.fori_loop(0, nq, q_block, 0)
    gk_ref[...] = gk_ref[...] * scale


def attn_bwd(lo, hi, q, k, v, do, o, lse, dqrow, dkcol, BQ=256, BK=256, mode=0):
    R, C = q.shape
    pairs = C // 128
    blk = pl.BlockSpec((R, 128), lambda p, *_: (0, p))
    f32 = jax.ShapeDtypeStruct((R, C), jnp.float32)
    return pl.pallas_call(
        functools.partial(attn_bwd_body, BQ, BK, mode),
        out_shape=(f32, f32, f32),
        grid_spec=pltpu.PrefetchScalarGridSpec(
            num_scalar_prefetch=2, grid=(pairs,),
            in_specs=[blk] * 6 + [pl.BlockSpec((1, R), lambda p, *_: (0, 0)), pl.BlockSpec((R, 1), lambda p, *_: (0, 0))],
            out_specs=[blk, blk, blk],
            scratch_shapes=[pltpu.VMEM((8, 128), jnp.float32)] * 3),
        cost_estimate=pl.CostEstimate(flops=pairs * 2 * R * R * 64 * 10, bytes_accessed=R * C * 24, transcendentals=pairs * 2 * R * R),
        name="attn_bwd",
    )(lo, hi, q, k, v, do, o, lse, dqrow, dkcol)


def ranges(lens, R, BQ, BK):
    ends = jnp.cumsum(lens)
    rid = jnp.arange(R)
    passed = (rid[:, None] >= ends[None, :]).astype(jnp.int32)
    doc = jnp.sum(passed, 1)
    st = jnp.sum(passed * lens[None, :], 1)
    en = jnp.sum(jnp.where(doc[:, None] == jnp.arange(lens.shape[0])[None, :], ends[None, :], 0), 1)
    lo = st[::BQ] // BK
    hi = (en[BQ - 1::BQ] + BK - 1) // BK
    return doc, (rid - st).astype(jnp.float32), lo.astype(jnp.int32), hi.astype(jnp.int32)


F32 = jnp.float32
BF16 = jnp.bfloat16
SWAP = [(0, 1), (1, 0)]


def swap(values, axis):
    return lax.ppermute(values, axis, SWAP)


def rope_tables(positions):
    lane = jnp.arange(128, dtype=jnp.int32)
    frequency = jnp.exp((lane % 32).astype(F32) * (-2.0 * math.log(rope_base) / HEAD_DIM))
    angles = positions[:, None] * frequency[None, :]
    sign = jnp.where(lane % 64 < 32, -1.0, 1.0).astype(F32)
    return jnp.cos(angles), jnp.sin(angles) * sign[None, :]


def rotate(values, cosine, sine):
    rows, width = values.shape
    parts = values.reshape(rows, width // 64, 2, 32)
    turned = jnp.stack([parts[:, :, 1], parts[:, :, 0]], axis=2).reshape(rows, width)
    tiles = width // 128
    return values * jnp.tile(cosine, (1, tiles)) + turned * jnp.tile(sine, (1, tiles))


def layer_norm(summed, gain_row, bias_row):
    centred = summed - jnp.mean(summed, axis=-1, keepdims=True)
    inv_std = lax.rsqrt(jnp.mean(centred * centred, axis=-1, keepdims=True) + norm_eps)
    normed = centred * inv_std
    return (normed * gain_row + bias_row, normed, inv_std)


def norm_back(grad_out, normed, inv_std, gain_row):
    e = grad_out * gain_row
    return inv_std * (
        e - jnp.mean(e, axis=-1, keepdims=True) - normed * jnp.mean(e * normed, axis=-1, keepdims=True)
    )


def dot(a, b, dims):
    return lax.dot_general(a, b, (dims, ((), ())), preferred_element_type=F32)


def both(partial):
    partial = partial.astype(BF16)
    other = swap(partial, "core")
    return partial.astype(F32) + other.astype(F32)


def forward_layer(x, xb, mats, norm_rows, tables, ids):
    wq, wo, wg, wd = mats
    lo, hi, col, row = ids
    width = wo.shape[1]
    projected = dot(xb, wq, ((1,), (0,)))
    q = rotate(projected[:, :width], *tables).astype(BF16)
    k = rotate(projected[:, width : 2 * width], *tables).astype(BF16)
    v = projected[:, 2 * width :].astype(BF16)
    o, lse = attn_fwd(lo, hi, q, k, v, col, row, 512, 512)
    a = both(dot(o, wo, ((1,), (1,))))
    h, n1, r1 = layer_norm(x + a, norm_rows[0], norm_rows[1])
    hb = h.astype(BF16)
    half = wd.shape[1]
    gate_up = dot(hb, wg, ((1,), (0,)))
    m = (jax.nn.silu(gate_up[:, :half]) * gate_up[:, half:]).astype(BF16)
    f = both(dot(m, wd, ((1,), (1,))))
    y, n2, r2 = layer_norm(h + f, norm_rows[2], norm_rows[3])
    return (xb, q, k, v, o, lse, n1, r1, hb, gate_up, m, n2, r2), y


def backward_layer(dy, mats, norm_rows, kept, tables, ids):
    xb, q, k, v, o, lse, n1, r1, hb, gate_up, m, n2, r2 = kept
    wq, wo, wg, wd = mats
    lo, hi, col, row = ids
    half = wd.shape[1]
    gain2 = jnp.sum(dy * n2, axis=0)
    bias2 = jnp.sum(dy, axis=0)
    dz2 = norm_back(dy, n2, r2, norm_rows[2])
    dzb2 = dz2.astype(BF16)
    g_down = dot(dzb2, m, ((0,), (0,)))
    dm = dot(dzb2, wd, ((1,), (0,)))
    gate, up = gate_up[:, :half], gate_up[:, half:]
    sig = jax.nn.sigmoid(gate)
    dub = jnp.concatenate(
        [dm * up * sig * (1.0 + gate * (1.0 - sig)), dm * gate * sig], axis=1
    ).astype(BF16)
    g_gate = dot(hb, dub, ((0,), (0,)))
    dh = both(dot(dub, wg, ((1,), (1,)))) + dz2
    gain1 = jnp.sum(dh * n1, axis=0)
    bias1 = jnp.sum(dh, axis=0)
    dz1 = norm_back(dh, n1, r1, norm_rows[0])
    dzb1 = dz1.astype(BF16)
    g_proj = dot(dzb1, o, ((0,), (0,)))
    do = dot(dzb1, wo, ((1,), (0,))).astype(BF16)
    gq, gk, gv = attn_bwd(lo, hi, q, k, v, do, o, lse, row, col, 512, 512)
    cosine, sine = tables
    dpb = jnp.concatenate([rotate(gq, cosine, -sine), rotate(gk, cosine, -sine), gv], axis=1).astype(BF16)
    g_qkv = dot(xb, dpb, ((0,), (0,)))
    dx = both(dot(dpb, wq, ((1,), (1,)))) + dz1
    return (g_qkv, g_proj, g_gate, g_down), jnp.stack([gain1, bias1, gain2, bias2]), dx


def update(weight, gradient, moment, average, rate):
    moment_new = keep_rate * moment + gradient
    weight_new = weight - rate * (gradient + keep_rate * moment_new)
    average_new = keep_rate * average + (1.0 - keep_rate) * weight_new
    return (gradient, weight_new, moment_new, average_new)


def gather(shard):
    own = lax.all_gather(shard, ("z", "y"), axis=0, tiled=True)
    return own, swap(own, "tx")


def pick(values, index, axis):
    return lax.dynamic_index_in_dim(values, index, axis, keepdims=False)


def halves(sheet, rows, y):
    laid = sheet.reshape(-1, 2, rows, sheet.shape[-1])
    return pick(laid, y, 1), pick(laid, 1 - y, 1)


def scatter_x(own, other, rows):
    y = lax.axis_index("y")
    got = swap(other.astype(BF16), "tx")
    keep, send = halves(own.astype(F32) + got.astype(F32), rows, y)
    got = swap(send.astype(BF16), "y")
    total = (keep + got.astype(F32)).astype(BF16)
    return lax.psum_scatter(total.reshape(-1, total.shape[-1]), "z", scatter_dimension=0, tiled=True).astype(F32)


def scatter_y(own, other, rows):
    y = lax.axis_index("y")
    keep_own, send_own = halves(own.astype(F32), rows, y)
    keep_other, send_other = halves(other.astype(F32), rows, y)
    got = swap(jnp.stack([send_own, send_other]).astype(BF16), "y").astype(F32)
    far = swap((keep_other + got[1]).astype(BF16), "tx").astype(F32)
    total = (keep_own + got[0] + far).astype(BF16)
    return lax.psum_scatter(total.reshape(-1, total.shape[-1]), "z", scatter_dimension=0, tiled=True).astype(F32)


def per_device(
    hidden_in, cotangent, lengths, deal, inverse, micro,
    qkv_weight, proj_weight, gate_up_weight, down_weight, norm_params,
    qkv_momentum, proj_momentum, gate_up_momentum, down_momentum, norm_momentum,
    qkv_average, proj_average, gate_up_average, down_average, norm_average,
):
    layers, rows = qkv_weight.shape[:2]
    heads_w = proj_weight.shape[2]
    hid_w = down_weight.shape[2]
    batches = micro.shape[1]
    local_rows, width = hidden_in.shape
    group_rows = deal.shape[0]
    pack_rows = group_rows // batches
    tx = lax.axis_index("tx")
    core = lax.axis_index("core")
    group_base = (lax.axis_index("z") * 2 + lax.axis_index("y")) * group_rows

    def four(block):
        pair = jnp.concatenate([block, swap(block, "tx")], axis=0)
        return jnp.concatenate([pair, swap(pair, "core")], axis=0)

    pack = lax.dynamic_index_in_dim(micro[0], tx, 0, keepdims=False)
    wanted = lax.dynamic_slice_in_dim(deal, pack * pack_rows, pack_rows, 0) - group_base
    block = wanted // local_rows
    place = jnp.where(block % 2 != core, 2, 0) + jnp.where(block // 2 != tx, 1, 0)
    source = place * local_rows + wanted % local_rows
    xb = four(hidden_in)[source]

    lens = lax.dynamic_index_in_dim(lengths[0], tx, 0, keepdims=False)
    doc, positions, lo, hi = ranges(lens, pack_rows, 512, 512)
    ids = (lo, hi, doc[:, None], doc[None, :])
    tables = rope_tables(positions)

    mats = []
    for i in range(layers):
        qkv, proj = qkv_weight[i], proj_weight[i]
        sheets = gather(jnp.concatenate([qkv.reshape(rows, 3 * heads_w), proj], axis=1).astype(BF16))
        gates = gather(gate_up_weight[i].reshape(rows, 2 * hid_w).astype(BF16))
        downs = gather(down_weight[i].astype(BF16))

        def side(w, first, count, each):
            return jnp.concatenate(
                [w[t][:, (first + c) * each : (first + c + 1) * each] for c in range(count) for t in range(2)], axis=1
            )

        mats.append((
            side(sheets, 0, 3, heads_w), side(sheets, 3, 1, heads_w), side(gates, 0, 2, hid_w), side(downs, 0, 1, hid_w)
        ))

    x = xb.astype(F32)
    stash = []
    for i in range(layers):
        kept, x = forward_layer(x, xb, mats[i], norm_params[i], tables, ids)
        xb = x.astype(BF16)
        stash.append(kept)

    def arrivals(values):
        half = pack_rows // 2
        mine = lax.dynamic_slice_in_dim(values, core * half, half, 0)
        far = swap(mine, "tx")
        near = swap(far, "core")
        other = jnp.where(core == 0, jnp.concatenate([far, near]), jnp.concatenate([near, far]))
        slots = lax.dynamic_slice_in_dim(inverse, (tx * 2 + core) * local_rows, local_rows, 0) - group_base
        held = slots // pack_rows == pack
        at = jnp.where(held, 0, pack_rows) + slots % pack_rows
        return jnp.concatenate([values, other])[at].astype(F32)

    block_out = arrivals(xb)

    grad = four(cotangent)[source].astype(F32)
    shares = [None] * layers
    norm_sums = [None] * layers
    for i in range(layers - 1, -1, -1):
        (g_qkv, g_proj, g_gate, g_down), norm_sums[i], grad = backward_layer(
            grad, mats[i], norm_params[i], stash[i], tables, ids
        )

        def sides(g, count, each):
            return [
                jnp.concatenate([g[:, (2 * c + t) * each : (2 * c + t + 1) * each] for c in range(count)], axis=1)
                for t in range(2)
            ]

        gu, dn = sides(g_gate, 2, hid_w), sides(g_down, 1, hid_w)
        qk, pr = sides(g_qkv, 3, heads_w), sides(g_proj, 1, heads_w)
        share_d = scatter_y(dn[0], dn[1], rows)
        share_g = scatter_x(gu[0], gu[1], rows)
        share_a = scatter_y(*[jnp.concatenate([qk[t], pr[t]], axis=1) for t in range(2)], rows)
        shares[i] = (
            share_a[:, : 3 * heads_w].reshape(rows, 3, heads_w),
            share_a[:, 3 * heads_w :],
            share_g.reshape(rows, 2, hid_w),
            share_d,
        )
    input_grad = arrivals(grad.astype(BF16))
    norm_total = lax.psum(0.5 * jnp.stack(norm_sums), ("z", "y", "tx", "core"))

    total_tokens = local_rows * 8 * lax.axis_size("z")
    proj_fan = max(1, D * 8 // SEQ_MOST)
    grads = [jnp.stack([shares[i][w] for i in range(layers)]) for w in range(4)]
    states = (
        update(qkv_weight, grads[0], qkv_momentum, qkv_average, step_size / math.sqrt(total_tokens * D)),
        update(proj_weight, grads[1], proj_momentum, proj_average, step_size / math.sqrt(total_tokens * proj_fan)),
        update(gate_up_weight, grads[2], gate_up_momentum, gate_up_average, step_size / math.sqrt(total_tokens * D)),
        update(down_weight, grads[3], down_momentum, down_average, step_size / math.sqrt(total_tokens * FF)),
        update(norm_params, norm_total, norm_momentum, norm_average, norm_step / math.sqrt(total_tokens)),
    )
    return (block_out, input_grad) + tuple(v for s in states for v in s)


def solution(mesh):
    dp, tensor = mesh.devices.shape
    fine = Mesh(mesh.devices.reshape(dp // 2, 2, 2, tensor // 2), ("z", "y", "tx", "core"))
    G, T = ("z", "y"), ("tx", "core")
    row = P(G + T, None)
    w4 = P(None, G, None, T)
    w3 = P(None, G, T)
    state = (w4, w3, w4, w3, P())
    placed = (row, row, P(G, None, None), P(G), P(G), P(G, None)) + state * 3
    outs = (row, row) + (w4,) * 4 + (w3,) * 4 + (w4,) * 4 + (w3,) * 4 + (P(),) * 4
    return jax.shard_map(per_device, mesh=fine, in_specs=placed, out_specs=outs, check_vma=False)
```

```python
import functools
import math

import jax
import jax.numpy as jnp
from jax import lax
from jax.experimental import pallas as pl
from jax.experimental.pallas import tpu as pltpu
from jax.sharding import Mesh, PartitionSpec as P

D = 768
HEAD_DIM = 64
FF = 3072
SEQ_MOST = 1024

norm_eps = 1e-05
rope_base = 1000.0
step_size = 2.0
norm_step = 0.1
keep_rate = 0.5
SCALE2 = HEAD_DIM ** (-0.5) * math.log2(math.e)
NT = (((1,), (1,)), ((), ()))
NN = (((1,), (0,)), ((), ()))
TN = (((0,), (0,)), ((), ()))


def mm(a, b, dims):
    return lax.dot_general(a, b, dims, preferred_element_type=jnp.float32)


def turn(values, cosine, sine):
    lane = lax.broadcasted_iota(jnp.int32, values.shape, 1)
    turned = jnp.where(lane % HEAD_DIM < 32, pltpu.roll(values, 96, 1), pltpu.roll(values, 32, 1))
    return values * cosine + turned * sine


def attn_fwd_body(BQ, BK, lo_ref, hi_ref, pq_ref, pk_ref, pv_ref, cos_ref, sin_ref, dq_ref, dk_ref,
                  q_ref, k_ref, v_ref, o_ref, lse_ref):
    R = q_ref.shape[0]

    def rope_block(i, _):
        rows = pl.ds(pl.multiple_of(i * 256, 256), 256)
        cosine, sine = cos_ref[rows, :], sin_ref[rows, :]
        q_ref[rows, :] = turn(pq_ref[rows, :], cosine, sine).astype(jnp.bfloat16)
        k_ref[rows, :] = turn(pk_ref[rows, :], cosine, sine).astype(jnp.bfloat16)
        v_ref[rows, :] = pv_ref[rows, :].astype(jnp.bfloat16)
        return 0

    lax.fori_loop(0, R // 256, rope_block, 0)
    lane = lax.broadcasted_iota(jnp.int32, (BQ, 128), 1)
    first = lane < HEAD_DIM
    zero = jnp.zeros((BQ, 128), jnp.bfloat16)

    def q_block(i, _):
        rows = pl.ds(pl.multiple_of(i * BQ, BQ), BQ)
        q = q_ref[rows, :]
        qs = (jnp.where(first, q, zero), jnp.where(first, zero, q))
        dq = dq_ref[rows, :]

        def kv_block(j, carry):
            cols = pl.ds(pl.multiple_of(j * BK, BK), BK)
            k = k_ref[cols, :]
            v = v_ref[cols, :]
            same = dq == dk_ref[:, cols]
            out = []
            for h in range(2):
                m, l, acc = carry[h]
                s = mm(qs[h], k, NT) * SCALE2
                s = jnp.where(same, s, -1e30)
                m_new = jnp.maximum(m, jnp.max(s, axis=1, keepdims=True))
                alpha = jnp.exp2(m - m_new)
                p = jnp.exp2(s - m_new)
                l = alpha * l + jnp.sum(p, axis=1, keepdims=True)
                acc = alpha * acc + mm(p.astype(jnp.bfloat16), v, NN)
                out.append((m_new, l, acc))
            return tuple(out)

        start = tuple(
            (jnp.full((BQ, 1), -2e30, jnp.float32), jnp.zeros((BQ, 1), jnp.float32), jnp.zeros((BQ, 128), jnp.float32))
            for h in range(2)
        )
        (m0, l0, a0), (m1, l1, a1) = lax.fori_loop(lo_ref[i], hi_ref[i], kv_block, start)
        o_ref[rows, :] = jnp.where(first, a0 / l0, a1 / l1).astype(jnp.bfloat16)
        lse_ref[rows, :] = jnp.where(first, m0 + jnp.log2(l0), m1 + jnp.log2(l1))
        return 0

    lax.fori_loop(0, R // BQ, q_block, 0)


def attn_fwd(lo, hi, projected, tables, dq, dk, BQ=256, BK=256):
    R = projected.shape[0]
    C = projected.shape[1] // 3
    pairs = C // 128
    blk = pl.BlockSpec((R, 128), lambda p, *_: (0, p))
    part = [pl.BlockSpec((R, 128), lambda p, *_, w=w: (0, w * pairs + p)) for w in range(3)]
    fixed = pl.BlockSpec((R, 128), lambda p, *_: (0, 0))
    half = jax.ShapeDtypeStruct((R, C), jnp.bfloat16)
    return pl.pallas_call(
        functools.partial(attn_fwd_body, BQ, BK),
        out_shape=(half, half, half, half, jax.ShapeDtypeStruct((R, C), jnp.float32)),
        grid_spec=pltpu.PrefetchScalarGridSpec(
            num_scalar_prefetch=2, grid=(pairs,),
            in_specs=part + [fixed, fixed, pl.BlockSpec((R, 1), lambda p, *_: (0, 0)), pl.BlockSpec((1, R), lambda p, *_: (0, 0))],
            out_specs=[blk] * 5),
        cost_estimate=pl.CostEstimate(flops=pairs * 2 * R * R * 64 * 4, bytes_accessed=R * C * 24, transcendentals=pairs * 2 * R * R),
        name="attn_fwd",
    )(lo, hi, projected, projected, projected, *tables, dq, dk)


def attn_bwd_body(BQ, BK, lo_ref, hi_ref, q_ref, k_ref, v_ref, do_ref, o_ref, lse_ref, cos_ref, sin_ref, dq_ref, dk_ref,
                  gq_out, gk_out, gv_out, gk_ref, gv_ref):
    R = q_ref.shape[0]
    nq = R // BQ
    scale = HEAD_DIM ** (-0.5)
    gk_ref[...] = jnp.zeros((R, 128), jnp.float32)
    gv_ref[...] = jnp.zeros((R, 128), jnp.float32)
    fq = lax.broadcasted_iota(jnp.int32, (BQ, 128), 1) < HEAD_DIM
    fk = lax.broadcasted_iota(jnp.int32, (BK, 128), 1) < HEAD_DIM
    zq = jnp.zeros((BQ, 128), jnp.bfloat16)
    zk = jnp.zeros((BK, 128), jnp.bfloat16)

    def q_block(i, _):
        rows = pl.ds(pl.multiple_of(i * BQ, BQ), BQ)
        q = q_ref[rows, :]
        do = do_ref[rows, :]
        prod = do.astype(jnp.float32) * o_ref[rows, :].astype(jnp.float32)
        lse_t = lse_ref[rows, :].T
        prod_t = prod.T
        qs = (jnp.where(fq, q, zq), jnp.where(fq, zq, q))
        dos = (jnp.where(fq, do, zq), jnp.where(fq, zq, do))
        lses = (lse_t[0:1, :], lse_t[64:65, :])
        deltas = (jnp.sum(prod_t[:64, :], axis=0, keepdims=True), jnp.sum(prod_t[64:, :], axis=0, keepdims=True))
        dq = dq_ref[:, rows]

        def kv_block(j, acc):
            cols = pl.ds(pl.multiple_of(j * BK, BK), BK)
            k = k_ref[cols, :]
            v = v_ref[cols, :]
            same = dk_ref[cols, :] == dq
            gk = gk_ref[cols, :]
            gv = gv_ref[cols, :]
            ks = (jnp.where(fk, k, zk), jnp.where(fk, zk, k))
            for h in range(2):
                s = mm(k, qs[h], NT) * SCALE2
                p = jnp.exp2(jnp.where(same, s - lses[h], -1e30))
                dp = mm(v, dos[h], NT)
                ds = (p * (dp - deltas[h])).astype(jnp.bfloat16)
                gv = gv + mm(p.astype(jnp.bfloat16), dos[h], NN)
                gk = gk + mm(ds, qs[h], NN)
                acc = acc + mm(ds, ks[h], TN)
            gk_ref[cols, :] = gk
            gv_ref[cols, :] = gv
            return acc

        gq = lax.fori_loop(lo_ref[i], hi_ref[i], kv_block, jnp.zeros((BQ, 128), jnp.float32)) * scale
        gq_out[rows, :] = turn(gq, cos_ref[rows, :], -sin_ref[rows, :]).astype(jnp.bfloat16)
        return 0

    lax.fori_loop(0, nq, q_block, 0)

    def close_block(i, _):
        rows = pl.ds(pl.multiple_of(i * 256, 256), 256)
        gk = gk_ref[rows, :] * scale
        gk_out[rows, :] = turn(gk, cos_ref[rows, :], -sin_ref[rows, :]).astype(jnp.bfloat16)
        gv_out[rows, :] = gv_ref[rows, :].astype(jnp.bfloat16)
        return 0

    lax.fori_loop(0, R // 256, close_block, 0)


def attn_bwd(lo, hi, q, k, v, do, o, lse, tables, dqrow, dkcol, BQ=256, BK=256):
    R, C = q.shape
    pairs = C // 128
    blk = pl.BlockSpec((R, 128), lambda p, *_: (0, p))
    fixed = pl.BlockSpec((R, 128), lambda p, *_: (0, 0))
    half = jax.ShapeDtypeStruct((R, C), jnp.bfloat16)
    return pl.pallas_call(
        functools.partial(attn_bwd_body, BQ, BK),
        out_shape=(half, half, half),
        grid_spec=pltpu.PrefetchScalarGridSpec(
            num_scalar_prefetch=2, grid=(pairs,),
            in_specs=[blk] * 6 + [fixed, fixed, pl.BlockSpec((1, R), lambda p, *_: (0, 0)), pl.BlockSpec((R, 1), lambda p, *_: (0, 0))],
            out_specs=[blk, blk, blk],
            scratch_shapes=[pltpu.VMEM((R, 128), jnp.float32)] * 2),
        cost_estimate=pl.CostEstimate(flops=pairs * 2 * R * R * 64 * 10, bytes_accessed=R * C * 24, transcendentals=pairs * 2 * R * R),
        name="attn_bwd",
    )(lo, hi, q, k, v, do, o, lse, *tables, dqrow, dkcol)


def ranges(lens, R, BQ, BK):
    ends = jnp.cumsum(lens)
    rid = jnp.arange(R)
    passed = (rid[:, None] >= ends[None, :]).astype(jnp.int32)
    doc = jnp.sum(passed, 1)
    st = jnp.sum(passed * lens[None, :], 1)
    en = jnp.sum(jnp.where(doc[:, None] == jnp.arange(lens.shape[0])[None, :], ends[None, :], 0), 1)
    lo = st[::BQ] // BK
    hi = (en[BQ - 1::BQ] + BK - 1) // BK
    return doc, (rid - st).astype(jnp.float32), lo.astype(jnp.int32), hi.astype(jnp.int32)


F32 = jnp.float32
BF16 = jnp.bfloat16
SWAP = [(0, 1), (1, 0)]


def swap(values, axis):
    return lax.ppermute(values, axis, SWAP)


def rope_tables(positions):
    lane = jnp.arange(128, dtype=jnp.int32)
    frequency = jnp.exp((lane % 32).astype(F32) * (-2.0 * math.log(rope_base) / HEAD_DIM))
    angles = positions[:, None] * frequency[None, :]
    sign = jnp.where(lane % 64 < 32, -1.0, 1.0).astype(F32)
    return jnp.cos(angles), jnp.sin(angles) * sign[None, :]


def layer_norm(summed, gain_row, bias_row):
    centred = summed - jnp.mean(summed, axis=-1, keepdims=True)
    inv_std = lax.rsqrt(jnp.mean(centred * centred, axis=-1, keepdims=True) + norm_eps)
    normed = centred * inv_std
    return (normed * gain_row + bias_row, normed, inv_std)


def norm_back(grad_out, normed, inv_std, gain_row):
    e = grad_out * gain_row
    return inv_std * (
        e - jnp.mean(e, axis=-1, keepdims=True) - normed * jnp.mean(e * normed, axis=-1, keepdims=True)
    )


def dot(a, b, dims):
    return lax.dot_general(a, b, (dims, ((), ())), preferred_element_type=F32)


def both(partial):
    partial = partial.astype(BF16)
    other = swap(partial, "core")
    return partial.astype(F32) + other.astype(F32)


def forward_layer(x, xb, mats, norm_rows, tables, ids):
    wq, wo, wg, wd = mats
    lo, hi, col, row = ids
    projected = dot(xb, wq, ((1,), (0,)))
    q, k, v, o, lse = attn_fwd(lo, hi, projected, tables, col, row, 512, 512)
    a = both(dot(o, wo, ((1,), (1,))))
    h, n1, r1 = layer_norm(x + a, norm_rows[0], norm_rows[1])
    hb = h.astype(BF16)
    half = wd.shape[1]
    gate_up = dot(hb, wg, ((1,), (0,)))
    m = (jax.nn.silu(gate_up[:, :half]) * gate_up[:, half:]).astype(BF16)
    f = both(dot(m, wd, ((1,), (1,))))
    y, n2, r2 = layer_norm(h + f, norm_rows[2], norm_rows[3])
    return (xb, q, k, v, o, lse, n1, r1, hb, gate_up, m, n2, r2), y


def backward_layer(dy, mats, norm_rows, kept, tables, ids):
    xb, q, k, v, o, lse, n1, r1, hb, gate_up, m, n2, r2 = kept
    wq, wo, wg, wd = mats
    lo, hi, col, row = ids
    half = wd.shape[1]
    gain2 = jnp.sum(dy * n2, axis=0)
    bias2 = jnp.sum(dy, axis=0)
    dz2 = norm_back(dy, n2, r2, norm_rows[2])
    dzb2 = dz2.astype(BF16)
    g_down = dot(dzb2, m, ((0,), (0,)))
    dm = dot(dzb2, wd, ((1,), (0,)))
    gate, up = gate_up[:, :half], gate_up[:, half:]
    sig = jax.nn.sigmoid(gate)
    dub = jnp.concatenate(
        [dm * up * sig * (1.0 + gate * (1.0 - sig)), dm * gate * sig], axis=1
    ).astype(BF16)
    g_gate = dot(hb, dub, ((0,), (0,)))
    dh = both(dot(dub, wg, ((1,), (1,)))) + dz2
    gain1 = jnp.sum(dh * n1, axis=0)
    bias1 = jnp.sum(dh, axis=0)
    dz1 = norm_back(dh, n1, r1, norm_rows[0])
    dzb1 = dz1.astype(BF16)
    g_proj = dot(dzb1, o, ((0,), (0,)))
    do = dot(dzb1, wo, ((1,), (0,))).astype(BF16)
    dpb = jnp.concatenate(attn_bwd(lo, hi, q, k, v, do, o, lse, tables, row, col, 512, 512), axis=1)
    g_qkv = dot(xb, dpb, ((0,), (0,)))
    dx = both(dot(dpb, wq, ((1,), (1,)))) + dz1
    return (g_qkv, g_proj, g_gate, g_down), jnp.stack([gain1, bias1, gain2, bias2]), dx


def update(weight, gradient, moment, average, rate):
    moment_new = keep_rate * moment + gradient
    weight_new = weight - rate * (gradient + keep_rate * moment_new)
    average_new = keep_rate * average + (1.0 - keep_rate) * weight_new
    return (gradient, weight_new, moment_new, average_new)


def spread(values, widths):
    far = swap(values, "tx")
    cols, at = [], 0
    for w in widths:
        cols += [values[:, at : at + w], far[:, at : at + w]]
        at += w
    return lax.all_gather(jnp.concatenate(cols, axis=1), ("z", "y"), axis=0, tiled=True)


def owners(partial, widths):
    share = lax.psum_scatter(partial, ("z", "y"), scatter_dimension=0, tiled=True)
    own, other, at = [], [], 0
    for w in widths:
        own.append(share[:, at : at + w])
        other.append(share[:, at + w : at + 2 * w])
        at += 2 * w
    got = swap(jnp.concatenate(other, axis=1), "tx")
    return jnp.concatenate(own, axis=1).astype(F32) + got.astype(F32)


def total_over(values):
    for axis in ("tx", "y"):
        values = values + swap(values, axis)
    count = lax.axis_size("z")
    if count & (count - 1):
        return lax.psum(values, "z")
    step = 1
    while step < count:
        values = values + lax.ppermute(values, "z", [(i, i ^ step) for i in range(count)])
        step *= 2
    return values


def per_device(
    hidden_in, cotangent, lengths, deal, inverse, micro,
    qkv_weight, proj_weight, gate_up_weight, down_weight, norm_params,
    qkv_momentum, proj_momentum, gate_up_momentum, down_momentum, norm_momentum,
    qkv_average, proj_average, gate_up_average, down_average, norm_average,
):
    layers, rows = qkv_weight.shape[:2]
    heads_w = proj_weight.shape[2]
    hid_w = down_weight.shape[2]
    batches = micro.shape[1]
    local_rows, width = hidden_in.shape
    group_rows = deal.shape[0]
    pack_rows = group_rows // batches
    tx = lax.axis_index("tx")
    core = lax.axis_index("core")
    group_base = (lax.axis_index("z") * 2 + lax.axis_index("y")) * group_rows

    def four(block):
        pair = jnp.concatenate([block, swap(block, "tx")], axis=0)
        return jnp.concatenate([pair, swap(pair, "core")], axis=0)

    pack = lax.dynamic_index_in_dim(micro[0], tx, 0, keepdims=False)
    wanted = lax.dynamic_slice_in_dim(deal, pack * pack_rows, pack_rows, 0) - group_base
    block = wanted // local_rows
    place = jnp.where(block % 2 != core, 2, 0) + jnp.where(block // 2 != tx, 1, 0)
    source = place * local_rows + wanted % local_rows
    xb = four(hidden_in)[source]

    lens = lax.dynamic_index_in_dim(lengths[0], tx, 0, keepdims=False)
    doc, positions, lo, hi = ranges(lens, pack_rows, 512, 512)
    ids = (lo, hi, doc[:, None], doc[None, :])
    tables = rope_tables(positions)

    mats = []
    for i in range(layers):
        heads = jnp.concatenate([qkv_weight[i].reshape(rows, 3 * heads_w), proj_weight[i]], axis=1).astype(BF16)
        hidden = jnp.concatenate([gate_up_weight[i].reshape(rows, 2 * hid_w), down_weight[i]], axis=1).astype(BF16)
        heads = spread(heads, [heads_w] * 4)
        hidden = spread(hidden, [hid_w] * 3)
        mats.append((heads[:, : 6 * heads_w], heads[:, 6 * heads_w :], hidden[:, : 4 * hid_w], hidden[:, 4 * hid_w :]))

    x = xb.astype(F32)
    stash = []
    for i in range(layers):
        kept, x = forward_layer(x, xb, mats[i], norm_params[i], tables, ids)
        xb = x.astype(BF16)
        stash.append(kept)

    def arrivals(values):
        half = pack_rows // 2
        mine = lax.dynamic_slice_in_dim(values, core * half, half, 0)
        far = swap(mine, "tx")
        near = swap(far, "core")
        other = jnp.where(core == 0, jnp.concatenate([far, near]), jnp.concatenate([near, far]))
        slots = lax.dynamic_slice_in_dim(inverse, (tx * 2 + core) * local_rows, local_rows, 0) - group_base
        held = slots // pack_rows == pack
        at = jnp.where(held, 0, pack_rows) + slots % pack_rows
        return jnp.concatenate([values, other])[at].astype(F32)

    block_out = arrivals(xb)

    grad = four(cotangent)[source].astype(F32)
    shares = [None] * layers
    norm_sums = [None] * layers
    for i in range(layers - 1, -1, -1):
        (g_qkv, g_proj, g_gate, g_down), norm_sums[i], grad = backward_layer(
            grad, mats[i], norm_params[i], stash[i], tables, ids
        )

        block = jnp.concatenate([g.astype(BF16) for g in (g_gate, g_down, g_proj)], axis=1)
        block = owners(block, [hid_w] * 3 + [heads_w])
        heads = owners(g_qkv.astype(BF16), [heads_w] * 3)
        shares[i] = (
            heads.reshape(rows, 3, heads_w),
            block[:, 3 * hid_w :],
            block[:, : 2 * hid_w].reshape(rows, 2, hid_w),
            block[:, 2 * hid_w : 3 * hid_w],
        )
    input_grad = arrivals(grad.astype(BF16))
    norm_total = total_over(jnp.stack(norm_sums))

    total_tokens = local_rows * 8 * lax.axis_size("z")
    proj_fan = max(1, D * 8 // SEQ_MOST)
    grads = [jnp.stack([shares[i][w] for i in range(layers)]) for w in range(4)]
    states = (
        update(qkv_weight, grads[0], qkv_momentum, qkv_average, step_size / math.sqrt(total_tokens * D)),
        update(proj_weight, grads[1], proj_momentum, proj_average, step_size / math.sqrt(total_tokens * proj_fan)),
        update(gate_up_weight, grads[2], gate_up_momentum, gate_up_average, step_size / math.sqrt(total_tokens * D)),
        update(down_weight, grads[3], down_momentum, down_average, step_size / math.sqrt(total_tokens * FF)),
        update(norm_params, norm_total, norm_momentum, norm_average, norm_step / math.sqrt(total_tokens)),
    )
    return (block_out, input_grad) + tuple(v for s in states for v in s)


def solution(mesh):
    dp, tensor = mesh.devices.shape
    fine = Mesh(mesh.devices.reshape(dp // 2, 2, 2, tensor // 2), ("z", "y", "tx", "core"))
    G, T = ("z", "y"), ("tx", "core")
    row = P(G + T, None)
    w4 = P(None, G, None, T)
    w3 = P(None, G, T)
    state = (w4, w3, w4, w3, P())
    placed = (row, row, P(G, None, None), P(G), P(G), P(G, None)) + state * 3
    outs = (row, row) + (w4,) * 4 + (w3,) * 4 + (w4,) * 4 + (w3,) * 4 + (P(),) * 4
    return jax.shard_map(per_device, mesh=fine, in_specs=placed, out_specs=outs, check_vma=False)
```
